32 devices in a mesh: tp: 4 (over y, x), rep: 8 (over z, core).
Axes of the slice: x: 2, y: 2, z: 4, core: 2. Of those that a mesh axis runs over, the one named last changes fastest.
Arguments:
- queries: bfloat16 [128, 4096], P('rep', 'tp'), may hold values from -6 to 6
- new_keys: bfloat16 [128, 2048], P('rep', 'tp'), may hold values from -6 to 6
- new_values: bfloat16 [128, 2048], P('rep', 'tp'), may hold values from -6 to 6
- stored_keys: bfloat16 [128, 16, 128, 128], P('rep', 'tp'), may hold values from -6 to 6
- stored_values: bfloat16 [128, 16, 128, 128], P('rep', 'tp'), may hold values from -6 to 6
- lengths: int32 [128], P('rep'), may hold values from 1 to 128
- out_proj: bfloat16 [4096, 4608], P('tp', 'rep'), may hold values from -0.09375 to 0.09375
- residual: bfloat16 [128, 4608], P(None, 'rep'), may hold values from -4.5 to 4.5
- norm_gain: float32 [4608], replicated, may hold values from 0.1 to 1.9
- embedding: bfloat16 [256000, 4608], P(('tp', 'rep')), may hold values from -1.25 to 1.25
- targets: int32 [128], replicated, may hold values from 0 to 255999
- old_sums: float32 [128], P('rep'), may hold values from -3 to 0
- rewards: float32 [128], P('rep'), may hold values from -6 to 6
- group_ids: int32 [128], P('rep'), may hold values from 0 to 15, as said below
Outputs:
- logprob_sum: float32 [128], P('rep')
- advantage: float32 [128], P('rep')
The draws below stay inside these ranges and needn't reach their ends.
Inputs may be any that keep to these rules, and one draw needn't show every extreme that they name: `group_ids`: each id names exactly 8 continuations.
All inputs are finite; a program needn't handle non-finite values.
Results may differ from the reference program's by a relative error of at most 0.001.
Values may be sent and summed in bfloat16 or wider, within the bound.
A program may use at most 128 MiB of HBM per device.

```python
import math
import jax
import jax.numpy as jnp
from jax import lax

D = 4608
QUERY_HEADS = 32
KEY_VALUE_HEADS = 16
HEAD_SIZE = 128
VOCAB = 256000
GROUP = 8
CACHE_SLOTS = 128
SAMPLE_COUNT = 128
QW = 4096
KW = 2048
N_TP = 4
N_REP = 8


def draw_residual(key, part):
    first, second, third = jax.random.split(jax.random.fold_in(key, 11), 3)
    columns = jnp.arange(D, dtype=jnp.float32)
    rough = jnp.exp(jax.random.uniform(second, (D,), jnp.float32, math.log(0.7), math.log(1.4)))
    rows = jnp.exp(jax.random.uniform(third, (SAMPLE_COUNT, 1), jnp.float32, math.log(0.5), math.log(2.0)))
    base = jnp.clip(jax.random.normal(first, (SAMPLE_COUNT, D), jnp.float32), -4.0, 4.0)
    ramp = 0.04 * 10.0 ** (columns / D)
    return (base * (ramp * rough)[None, :] * rows).astype(jnp.bfloat16)


def draw_embedding(key, part):
    first, second = jax.random.split(jax.random.fold_in(key, 23), 2)
    rows = jnp.arange(VOCAB, dtype=jnp.float32) / VOCAB
    rough = jnp.exp(jax.random.uniform(second, (VOCAB,), jnp.float32, math.log(0.88), math.log(1.14)))
    base = jnp.clip(jax.random.normal(first, (VOCAB, D), jnp.float32), -4.0, 4.0)
    spread = jnp.sqrt(14.0 + 2.2 * rows)
    return (base * (spread * rough)[:, None] / math.sqrt(D)).astype(jnp.bfloat16)


def draw_group_ids(key, part):
    order = jax.random.permutation(jax.random.fold_in(key, 37), SAMPLE_COUNT)
    return (order // GROUP).astype(jnp.int32)


def touch_ends(values, key, low, high):
    spot = [jax.random.randint(jax.random.fold_in(key, axis), (), 0, length) for axis, length in enumerate(values.shape)]
    longest = values.shape.index(max(values.shape))
    neighbour = spot[:longest] + [(spot[longest] + 1) % values.shape[longest]] + spot[longest + 1:]
    return values.at[tuple(spot)].set(low).at[tuple(neighbour)].set(high)


def block_scale(rng, shape, cuts, smallest, largest):
    level, own = 1.0, jax.random.fold_in(rng, 6)
    for position, parts in cuts:
        steps = jnp.exp(jax.random.uniform(jax.random.fold_in(own, position), (parts,), jnp.float32, smallest / len(cuts), largest / len(cuts)))
        level = level * jnp.repeat(steps, shape[position] // parts).reshape([-1 if axis == position else 1 for axis in range(len(shape))])
    return level


def gaussian(rng, extent, deviation, reach, cuts=(), kind=jnp.bfloat16):
    drawn = deviation * jax.random.normal(rng, extent, jnp.float32)
    if cuts:
        drawn = drawn * block_scale(rng, extent, cuts, -0.22, 0.18)
    return jnp.clip(drawn, -reach, reach).astype(kind)


def setup_inputs(seed: int = 0) -> dict:
    arg_keys = jax.random.split(jax.random.key(seed), 15)
    return {
        "queries": gaussian(arg_keys[0], (SAMPLE_COUNT, QW), 1.0, 6.0, ((0, 8), (1, 4))),
        "new_keys": gaussian(arg_keys[1], (SAMPLE_COUNT, KW), 1.0, 6.0, ((0, 8), (1, 4))),
        "new_values": gaussian(arg_keys[2], (SAMPLE_COUNT, KW), 1.0, 6.0, ((0, 8), (1, 4))),
        "stored_keys": gaussian(arg_keys[3], (SAMPLE_COUNT, KEY_VALUE_HEADS, CACHE_SLOTS, HEAD_SIZE), 1.0, 6.0, ((0, 8), (1, 4))),
        "stored_values": gaussian(arg_keys[4], (SAMPLE_COUNT, KEY_VALUE_HEADS, CACHE_SLOTS, HEAD_SIZE), 1.0, 6.0, ((0, 8), (1, 4))),
        "lengths": touch_ends(jax.random.randint(arg_keys[5], (SAMPLE_COUNT,), 1, CACHE_SLOTS + 1), jax.random.fold_in(arg_keys[5], 1), 1, CACHE_SLOTS).astype(jnp.int32),
        "out_proj": gaussian(arg_keys[6], (QW, D), QW ** -0.5, 0.09375, ((0, 4), (1, 8))),
        "residual": draw_residual(jax.random.fold_in(arg_keys[14], 71), 0),
        "norm_gain": jnp.clip(1.0 + 0.18 * jax.random.normal(arg_keys[8], (D,), jnp.float32), 0.1, 1.9),
        "embedding": draw_embedding(jax.random.fold_in(arg_keys[14], 71), 0),
        "targets": touch_ends(jax.random.randint(arg_keys[10], (SAMPLE_COUNT,), 0, VOCAB), jax.random.fold_in(arg_keys[10], 1), 0, VOCAB - 1).astype(jnp.int32),
        "old_sums": jnp.clip(-3.0 + 3.0 * jax.random.uniform(arg_keys[11], (SAMPLE_COUNT,), jnp.float32) ** block_scale(arg_keys[11], (SAMPLE_COUNT,), ((0, 8),), -0.2, 0.2), -3.0, 0.0),
        "rewards": gaussian(arg_keys[12], (SAMPLE_COUNT,), 1.0, 6.0, ((0, 8),), jnp.float32),
        "group_ids": draw_group_ids(jax.random.fold_in(arg_keys[14], 71), 0),
    }


def attend_one(items):
    query_vector, fresh_key, fresh_value, keys, values, length = items
    sample_ratio = QUERY_HEADS // KEY_VALUE_HEADS
    query_float = query_vector.astype(jnp.float32).reshape(KEY_VALUE_HEADS, sample_ratio, HEAD_SIZE)
    scores = jnp.einsum('gqd,gpd->gqp', query_float, keys.astype(jnp.float32)) / 12.0
    scores = 50.0 * jnp.tanh(scores / 50.0)
    valid = jnp.arange(CACHE_SLOTS, dtype=jnp.int32) < length
    expo = jnp.where(valid[None, None, :], jnp.exp(scores), 0.0)
    own_logit = jnp.einsum('xvi,xi->xv', query_float, fresh_key.astype(jnp.float32).reshape(KEY_VALUE_HEADS, HEAD_SIZE)) / 12.0
    own_logit = 50.0 * jnp.tanh(own_logit / 50.0)
    own_exp = jnp.exp(own_logit)
    total = lax.optimization_barrier(jnp.sum(expo, -1)) + own_exp
    probs = (expo / total[..., None]).astype(jnp.bfloat16)
    own_probability = (own_exp / total).astype(jnp.bfloat16)
    attended_output = jnp.einsum('gqp,gpd->gqd', probs.astype(jnp.float32), values.astype(jnp.float32))
    attended_output = attended_output + own_probability.astype(jnp.float32)[..., None] * fresh_value.astype(jnp.float32).reshape(KEY_VALUE_HEADS, 1, HEAD_SIZE)
    return attended_output.reshape(QUERY_HEADS * HEAD_SIZE).astype(jnp.bfloat16)

def reference(queries, new_keys, new_values, stored_keys, stored_values, lengths, out_proj, residual, norm_gain, embedding, targets, old_sums, rewards, group_ids):
    context = lax.map(attend_one, (queries, new_keys, new_values, stored_keys, stored_values, lengths))
    stream = residual.astype(jnp.float32) + jnp.dot(context, out_proj, preferred_element_type=jnp.float32)
    scale = lax.rsqrt(lax.optimization_barrier(jnp.mean(stream * stream, axis=1, keepdims=True)) + 1e-06)
    normed = (stream * scale * norm_gain[None, :]).astype(jnp.bfloat16)
    pieces = N_TP * N_REP
    width = VOCAB // pieces
    blocks = embedding.reshape(pieces, width, D)
    starts = jnp.arange(pieces, dtype=jnp.int32) * width

    def visit(carry, item):
        total, picked = carry
        block, start = item
        logits = lax.dot_general(normed, block, (((1,), (1,)), ((), ())), preferred_element_type=jnp.float32)
        logits = 30.0 * jnp.tanh(logits / 30.0)
        ids = start + jnp.arange(width, dtype=jnp.int32)
        total = total + lax.optimization_barrier(jnp.sum(jnp.exp(logits), 1))
        picked = picked + lax.optimization_barrier(jnp.sum(jnp.where(ids[None, :] == targets[:, None], logits, 0.0), 1))
        return ((total, picked), None)
    zeros = jnp.zeros((SAMPLE_COUNT,), jnp.float32)
    (total, picked), _ = lax.scan(visit, (zeros, zeros), (blocks, starts))
    logprob_sum = old_sums + (picked - jnp.log(total))
    groups = SAMPLE_COUNT // GROUP
    member = group_ids[:, None] == jnp.arange(groups, dtype=jnp.int32)[None, :]
    totals = lax.optimization_barrier(jnp.sum(jnp.where(member, rewards[:, None], 0.0), 0))
    mine = lax.optimization_barrier(jnp.sum(jnp.where(member, totals[None, :], 0.0), 1))
    advantage = rewards - (mine - rewards) / (GROUP - 1.0)
    return (logprob_sum, advantage)
```

```python
import functools

import jax
import jax.numpy as jnp
from jax import lax
from jax.experimental import pallas as pl
from jax.experimental.pallas import tpu as pltpu
from jax.sharding import PartitionSpec as P

MESH = pl.DeviceIdType.MESH
ROWS_PER_BLOCK = 512
SLOTS = 10
VMEM_BYTES = 66 * 1000 * 1000

GROUP = 8


def attention(queries, new_keys, new_values, stored_keys, stored_values, lengths):
    samp, heads_kv, span, depth = stored_keys.shape
    sample_ratio = queries.shape[1] // (heads_kv * depth)
    query_vector = queries.reshape(samp, heads_kv, sample_ratio, depth)
    scores = (
        jnp.einsum("sgqd,sgpd->sgqp", query_vector, stored_keys, preferred_element_type=jnp.float32)
        / 12.0
    )
    scores = 50.0 * jnp.tanh(scores / 50.0)
    valid = lax.broadcasted_iota(jnp.int32, (samp, 1, 1, span), 3) < lengths[:, None, None, None]
    expo = jnp.where(valid, jnp.exp(scores), 0.0)
    own_logit = (
        jnp.einsum(
            "sgqd,sgd->sgq",
            query_vector,
            new_keys.reshape(samp, heads_kv, depth),
            preferred_element_type=jnp.float32,
        )
        / 12.0
    )
    own_logit = 50.0 * jnp.tanh(own_logit / 50.0)
    own_exp = jnp.exp(own_logit)
    total = jnp.sum(expo, -1) + own_exp
    probs = (expo / total[..., None]).astype(jnp.bfloat16)
    own_probability = (own_exp / total).astype(jnp.bfloat16)
    attended_output = jnp.einsum(
        "sgqp,sgpd->sgqd", probs, stored_values, preferred_element_type=jnp.float32
    )
    attended_output = attended_output + own_probability.astype(jnp.float32)[
        ..., None
    ] * new_values.reshape(samp, heads_kv, 1, depth).astype(jnp.float32)
    return attended_output.reshape(samp, sample_ratio * heads_kv * depth).astype(jnp.bfloat16)


def per_device(
    queries,
    new_keys,
    new_values,
    stored_keys,
    stored_values,
    lengths,
    out_proj,
    residual,
    norm_gain,
    embedding,
    targets,
    old_sums,
    rewards,
    group_ids,
):
    samp = queries.shape[0]
    reps = lax.axis_size("rep")
    rep_index = lax.axis_index("rep")
    tp_index = lax.axis_index("tp")
    groups = samp * reps // GROUP
    member = group_ids[:, None] == lax.broadcasted_iota(jnp.int32, (1, groups), 1)
    reward_part = jnp.sum(jnp.where(member, rewards[:, None], 0.0), 0)
    group_total = lax.psum(reward_part, "rep")
    mine = jnp.sum(jnp.where(member, group_total[None, :], 0.0), 1)
    advantage = rewards - (mine - rewards) / (GROUP - 1.0)
    context = attention(queries, new_keys, new_values, stored_keys, stored_values, lengths)
    partial_value = jnp.dot(
        lax.all_gather(context, "rep", axis=0, tiled=True),
        out_proj,
        preferred_element_type=jnp.float32,
    )
    vocab_rows = embedding.shape[0]
    contract = (((1,), (1,)), ((), ()))
    heads = lax.psum(partial_value, "tp")
    stream = residual.astype(jnp.float32) + heads
    full = lax.all_gather(stream, "rep", axis=1, tiled=True)
    scale = lax.rsqrt(jnp.mean(full * full, axis=1, keepdims=True) + 1e-06)
    normed = (full * scale * norm_gain[None, :]).astype(jnp.bfloat16)
    logits = lax.dot_general(normed, embedding, contract, preferred_element_type=jnp.float32)
    capped = 30.0 * jnp.tanh(logits / 30.0)
    offset = (tp_index * reps + rep_index) * vocab_rows
    entry_ids = offset + lax.broadcasted_iota(jnp.int32, (1, vocab_rows), 1)
    picked_part = jnp.sum(jnp.where(entry_ids == targets[:, None], capped, 0.0), 1)
    total, picked = lax.psum((jnp.sum(jnp.exp(capped), 1), picked_part), ("tp", "rep"))
    logprob = picked - jnp.log(total)
    own_rows = lax.dynamic_slice_in_dim(logprob, rep_index * samp, samp)
    logprob_sum = old_sums + own_rows
    return (logprob_sum, advantage)


def as_column(row, count):
    eye = lax.broadcasted_iota(jnp.int32, (count, count), 0) == lax.broadcasted_iota(
        jnp.int32, (count, count), 1
    )
    return jnp.sum(jnp.where(eye, row, 0.0), 1, keepdims=True)


def as_row(column, count):
    eye = lax.broadcasted_iota(jnp.int32, (count, count), 0) == lax.broadcasted_iota(
        jnp.int32, (count, count), 1
    )
    return jnp.sum(jnp.where(eye, column, 0.0), 0, keepdims=True)


def step_kernel(
    tps,
    reps,
    lengths,
    queries,
    new_keys,
    new_values,
    residual,
    gain,
    targets,
    old_sums,
    rewards,
    group_ids,
    keys_hbm,
    values_hbm,
    proj_hbm,
    table_hbm,
    logprob_out,
    advantage_out,
    keys,
    values,
    proj,
    table,
    q_rows,
    nk_rows,
    nv_rows,
    ctx_rows,
    context,
    partial,
    reduced,
    blocks,
    normed,
    reward_rows,
    final_tp,
    final_rep,
    local_sem,
    table_sem,
    send_sem,
    ctx_sem,
    red_sem,
    block_sem,
    reward_sem,
    ftp_sem,
    frep_sem,
):
    t = lax.axis_index("tp")
    r = lax.axis_index("rep")
    samp, heads_kv, span, depth = keys_hbm.shape
    heads = queries.shape[1] // depth
    ratio = heads // heads_kv
    total_samp = samp * reps
    cols = residual.shape[1]
    padded = blocks.shape[2]
    share = total_samp // tps
    vocab_rows, width = table_hbm.shape
    full = vocab_rows // ROWS_PER_BLOCK
    tail = vocab_rows - full * ROWS_PER_BLOCK
    zs = reps // 2
    core = lax.rem(r, 2)
    partner = r + 1 - 2 * core
    sent = []

    def table_copy(index, slot):
        return pltpu.make_async_copy(
            table_hbm.at[pl.ds(pl.multiple_of(index * ROWS_PER_BLOCK, ROWS_PER_BLOCK), ROWS_PER_BLOCK)],
            table.at[slot],
            table_sem.at[slot],
        )

    def tail_copy():
        slot = full % SLOTS
        return pltpu.make_async_copy(
            table_hbm.at[pl.ds(full * ROWS_PER_BLOCK, tail)],
            table.at[slot, pl.ds(0, tail)],
            table_sem.at[slot],
        )

    key_copies = [pltpu.make_async_copy(keys_hbm, keys, local_sem.at[0])]
    value_copies = [pltpu.make_async_copy(values_hbm, values, local_sem.at[1])]
    proj_copy = pltpu.make_async_copy(proj_hbm, proj, local_sem.at[2])
    for copy in key_copies + value_copies + [proj_copy]:
        copy.start()
    for index in range(SLOTS):
        table_copy(index, index).start()

    barrier = pltpu.get_barrier_semaphore()
    for k in range(1, tps):
        pl.semaphore_signal(
            barrier, inc=1, device_id=(lax.rem(t + k, tps), r), device_id_type=MESH
        )
    for k in range(1, reps):
        pl.semaphore_signal(
            barrier, inc=1, device_id=(t, lax.rem(r + k, reps)), device_id_type=MESH
        )

    def send(src, dst, recv, device):
        copy = pltpu.make_async_remote_copy(
            src_ref=src,
            dst_ref=dst,
            send_sem=send_sem.at[len(sent)],
            recv_sem=recv,
            device_id=device,
            device_id_type=MESH,
        )
        copy.start()
        sent.append(copy)

    def received(ref, recv):
        pltpu.make_async_remote_copy(
            src_ref=ref,
            dst_ref=ref,
            send_sem=send_sem.at[0],
            recv_sem=recv,
            device_id=(t, partner),
            device_id_type=MESH,
        ).wait_recv()

    reward_rows[r] = jnp.zeros(reward_rows.shape[1:], jnp.float32)
    reward_rows[r, 0:1, 0:samp] = rewards[...]
    reward_rows[r, 1:2, 0:samp] = group_ids[...].astype(jnp.float32)

    for h in range(heads):
        g = h // ratio
        q_rows[:, h, :] = queries[:, h * depth : (h + 1) * depth].astype(jnp.float32)
        nk_rows[:, h, :] = new_keys[:, g * depth : (g + 1) * depth].astype(jnp.float32)
        nv_rows[:, h, :] = new_values[:, g * depth : (g + 1) * depth].astype(jnp.float32)

    head_group = lax.broadcasted_iota(jnp.int32, (heads, span), 0) // ratio
    position = lax.broadcasted_iota(jnp.int32, (heads, span), 1)
    for copy in key_copies:
        copy.wait()
    probs = []
    own_probs = []
    for s in range(samp):
        query = q_rows[s]
        wide = lax.dot_general(
            query.astype(jnp.bfloat16),
            keys[s].reshape(heads_kv * span, depth),
            (((1,), (1,)), ((), ())),
            preferred_element_type=jnp.float32,
        )
        scores = wide[:, 0:span]
        for g in range(1, heads_kv):
            scores = jnp.where(head_group == g, wide[:, g * span : (g + 1) * span], scores)
        scores = 50.0 * jnp.tanh(scores / 12.0 / 50.0)
        expo = jnp.where(position < lengths[s], jnp.exp(scores), 0.0)
        own = jnp.sum(query * nk_rows[s], 1, keepdims=True) / 12.0
        own_exp = jnp.exp(50.0 * jnp.tanh(own / 50.0))
        total = jnp.sum(expo, 1, keepdims=True) + own_exp
        probs.append((expo / total).astype(jnp.bfloat16).astype(jnp.float32))
        own_probs.append((own_exp / total).astype(jnp.bfloat16).astype(jnp.float32))
    for copy in value_copies:
        copy.wait()
    for s in range(samp):
        spread = jnp.concatenate(
            [jnp.where(head_group == g, probs[s], 0.0) for g in range(heads_kv)], axis=1
        )
        attended = jnp.dot(
            spread.astype(jnp.bfloat16),
            values[s].reshape(heads_kv * span, depth),
            preferred_element_type=jnp.float32,
        )
        ctx_rows[s] = attended + own_probs[s] * nv_rows[s]
    own_ctx = context.at[pl.ds(pl.multiple_of(r * samp, samp), samp)]
    for h in range(heads):
        own_ctx[:, h * depth : (h + 1) * depth] = ctx_rows[:, h, :].astype(jnp.bfloat16)

    pl.semaphore_wait(barrier, tps + reps - 2)

    def ctx_slot(q):
        return context.at[pl.ds(pl.multiple_of(q * samp, samp), samp)]

    for k in range(1, zs):
        send(ctx_slot(r), ctx_slot(r), ctx_sem.at[r], (t, lax.rem(r + 2 * k, reps)))
    send(ctx_slot(r), ctx_slot(r), ctx_sem.at[r], (t, partner))
    for k in range(1, reps):
        send(reward_rows.at[r], reward_rows.at[r], reward_sem.at[r], (t, lax.rem(r + k, reps)))
    for k in range(1, zs):
        q = lax.rem(r + 2 * k, reps)
        received(ctx_slot(q), ctx_sem.at[q])
        send(ctx_slot(q), ctx_slot(q), ctx_sem.at[q], (t, partner))
    for k in range(zs):
        q = lax.rem(partner + 2 * k, reps)
        received(ctx_slot(q), ctx_sem.at[q])

    proj_copy.wait()
    product = jnp.dot(context[...], proj[...], preferred_element_type=jnp.float32)
    for k in range(tps):
        partial[k] = product[k * share : (k + 1) * share]
    for k in range(1, tps):
        u = lax.rem(t + k, tps)
        send(partial.at[u], reduced.at[t], red_sem.at[t], (u, r))
    reduced[t] = partial[t]
    own_gain = gain[:, 0:cols]
    for q in range(1, reps):
        own_gain = jnp.where(r == q, gain[:, q * cols : (q + 1) * cols], own_gain)
    rest = residual[pl.ds(pl.multiple_of(t * share, share), share)].astype(jnp.float32)
    for k in range(1, tps):
        u = lax.rem(t + k, tps)
        received(reduced.at[u], red_sem.at[u])
    stream = reduced[0]
    for k in range(1, tps):
        stream = stream + reduced[k]
    stream = stream + rest
    square = jnp.sum(stream * stream, 1, keepdims=True)
    high = square.astype(jnp.bfloat16).astype(jnp.float32)
    mid = (square - high).astype(jnp.bfloat16).astype(jnp.float32)
    low = square - high - mid
    lane = lax.broadcasted_iota(jnp.int32, (share, padded - cols), 1)
    extra = jnp.where(lane == 0, high, jnp.where(lane == 1, mid, jnp.where(lane == 2, low, 0.0)))
    mine = blocks.at[r, pl.ds(pl.multiple_of(t * share, share), share)]
    mine[:, 0:cols] = (stream * own_gain).astype(jnp.bfloat16)
    mine[:, cols:padded] = extra.astype(jnp.bfloat16)

    def block(u, q):
        return blocks.at[q, pl.ds(pl.multiple_of(u * share, share), share)]

    def arrived(u, q):
        return block_sem.at[u * reps + q]

    for k in range(1, zs):
        send(block(t, r), block(t, r), arrived(t, r), (t, lax.rem(r + 2 * k, reps)))
    for step in range(zs):
        q = lax.rem(r + 2 * step, reps)
        if step:
            received(block(t, q), arrived(t, q))
        for k in range(1, tps):
            send(block(t, q), block(t, q), arrived(t, q), (lax.rem(t + k, tps), r))
        send(block(t, q), block(t, q), arrived(t, q), (t, partner))
    for step in range(zs):
        q = lax.rem(r + 2 * step, reps)
        for k in range(1, tps):
            u = lax.rem(t + k, tps)
            received(block(u, q), arrived(u, q))
            send(block(u, q), block(u, q), arrived(u, q), (t, partner))
    for step in range(zs):
        q = lax.rem(partner + 2 * step, reps)
        for k in range(tps):
            u = lax.rem(t + k, tps)
            received(block(u, q), arrived(u, q))

    squares = jnp.zeros((total_samp, 1), jnp.float32)
    for z in range(zs):
        left = blocks[2 * z].astype(jnp.float32)
        right = blocks[2 * z + 1].astype(jnp.float32)
        pair = jnp.concatenate([left[:, 0:cols], right[:, 0:cols]], axis=1)
        normed[:, 2 * z * cols : 2 * (z + 1) * cols] = pair.astype(jnp.bfloat16)
        squares = squares + jnp.sum(left[:, cols:padded], 1, keepdims=True)
        squares = squares + jnp.sum(right[:, cols:padded], 1, keepdims=True)
    scale = lax.rsqrt(squares / width + 1e-06)
    wanted = as_column(targets[...].astype(jnp.float32), total_samp).astype(jnp.int32)
    wanted = wanted - (t * reps + r) * vocab_rows

    def score(rows, first, carry):
        total, picked = carry
        logits = lax.dot_general(
            normed[...], rows, (((1,), (1,)), ((), ())), preferred_element_type=jnp.float32
        )
        capped = 30.0 * jnp.tanh(logits * scale / 30.0)
        entry = lax.broadcasted_iota(jnp.int32, capped.shape, 1) + first
        total = total + jnp.sum(jnp.exp(capped), 1, keepdims=True)
        picked = picked + jnp.sum(jnp.where(entry == wanted, capped, 0.0), 1, keepdims=True)
        return total, picked

    def visit(index, carry):
        slot = lax.rem(index, SLOTS)
        table_copy(index, slot).wait()
        carry = score(table[slot], index * ROWS_PER_BLOCK, carry)

        @pl.when(index + SLOTS < full)
        def _():
            table_copy(index + SLOTS, slot).start()

        if tail:

            @pl.when(index + SLOTS == full)
            def _():
                tail_copy().start()

        return carry

    zero = jnp.zeros((total_samp, 1), jnp.float32)
    carry = lax.fori_loop(0, full, visit, (zero, zero))
    if tail:
        tail_copy().wait()
        carry = score(table[full % SLOTS, 0:tail], full * ROWS_PER_BLOCK, carry)

    final_tp[t] = jnp.zeros(final_tp.shape[1:], jnp.float32)
    final_tp[t, 0:1] = as_row(carry[0], total_samp)
    final_tp[t, 1:2] = as_row(carry[1], total_samp)
    for k in range(1, tps):
        send(final_tp.at[t], final_tp.at[t], ftp_sem.at[t], (lax.rem(t + k, tps), r))

    for k in range(1, reps):
        q = lax.rem(r + k, reps)
        received(reward_rows.at[q], reward_sem.at[q])
    own_ids = as_column(group_ids[...].astype(jnp.float32), samp)
    group_sum = jnp.zeros((samp, 1), jnp.float32)
    for q in range(reps):
        same = own_ids == reward_rows[q, 1:2, 0:samp]
        group_sum = group_sum + jnp.sum(
            jnp.where(same, reward_rows[q, 0:1, 0:samp], 0.0), 1, keepdims=True
        )
    group_sum = as_row(group_sum, samp)
    advantage_out[...] = rewards[...] - (group_sum - rewards[...]) / (GROUP - 1.0)

    for k in range(1, tps):
        u = lax.rem(t + k, tps)
        received(final_tp.at[u], ftp_sem.at[u])
    column = final_tp[0]
    for k in range(1, tps):
        column = column + final_tp[k]
    final_rep[r] = column
    for k in range(1, reps):
        send(final_rep.at[r], final_rep.at[r], frep_sem.at[r], (t, lax.rem(r + k, reps)))
    for k in range(1, reps):
        q = lax.rem(r + k, reps)
        received(final_rep.at[q], frep_sem.at[q])
    whole = final_rep[0]
    for k in range(1, reps):
        whole = whole + final_rep[k]
    logprob = whole[1:2] - jnp.log(whole[0:1])
    chosen = lax.broadcasted_iota(jnp.int32, (samp, total_samp), 1) == (
        lax.broadcasted_iota(jnp.int32, (samp, total_samp), 0) + r * samp
    )
    own_rows = jnp.sum(jnp.where(chosen, logprob, 0.0), 1, keepdims=True)
    logprob_out[...] = old_sums[...] + as_row(own_rows, samp)
    for copy in sent:
        copy.wait_send()


def one_kernel(
    queries,
    new_keys,
    new_values,
    stored_keys,
    stored_values,
    lengths,
    out_proj,
    residual,
    norm_gain,
    embedding,
    targets,
    old_sums,
    rewards,
    group_ids,
):
    tps, reps = lax.axis_size("tp"), lax.axis_size("rep")
    samp, heads_kv, span, depth = stored_keys.shape
    heads = queries.shape[1] // depth
    total_samp = samp * reps
    cols = out_proj.shape[1]
    padded = (cols + 3 + 127) // 128 * 128
    share = total_samp // tps
    zs = reps // 2
    sends = (
        (zs - 1) + zs + (reps - 1) + (tps - 1) + (zs - 1) + zs * (tps - 1) + zs * tps
        + (tps - 1) + (reps - 1)
    )
    vmem = pl.BlockSpec(memory_space=pltpu.VMEM)
    smem = pl.BlockSpec(memory_space=pltpu.SMEM)
    hbm = pl.BlockSpec(memory_space=pltpu.HBM)
    dma = pltpu.SemaphoreType.DMA
    logprob, advantage = pl.pallas_call(
        functools.partial(step_kernel, tps, reps),
        out_shape=[jax.ShapeDtypeStruct((1, samp), jnp.float32)] * 2,
        in_specs=[smem] + [vmem] * 9 + [hbm] * 4,
        out_specs=[vmem, vmem],
        scratch_shapes=[
            pltpu.VMEM(stored_keys.shape, stored_keys.dtype),
            pltpu.VMEM(stored_values.shape, stored_values.dtype),
            pltpu.VMEM(out_proj.shape, out_proj.dtype),
            pltpu.VMEM((SLOTS, ROWS_PER_BLOCK, embedding.shape[1]), embedding.dtype),
            pltpu.VMEM((samp, heads, depth), jnp.float32),
            pltpu.VMEM((samp, heads, depth), jnp.float32),
            pltpu.VMEM((samp, heads, depth), jnp.float32),
            pltpu.VMEM((samp, heads, depth), jnp.float32),
            pltpu.VMEM((total_samp, heads * depth), jnp.bfloat16),
            pltpu.VMEM((tps, share, cols), jnp.float32),
            pltpu.VMEM((tps, share, cols), jnp.float32),
            pltpu.VMEM((reps, total_samp, padded), jnp.bfloat16),
            pltpu.VMEM((total_samp, embedding.shape[1]), jnp.bfloat16),
            pltpu.VMEM((reps, 8, 128), jnp.float32),
            pltpu.VMEM((tps, 8, total_samp), jnp.float32),
            pltpu.VMEM((reps, 8, total_samp), jnp.float32),
            dma((3,)),
            dma((SLOTS,)),
            dma((sends,)),
            dma((reps,)),
            dma((tps,)),
            dma((tps * reps,)),
            dma((reps,)),
            dma((tps,)),
            dma((reps,)),
        ],
        compiler_params=pltpu.CompilerParams(
            collective_id=0, has_side_effects=True, vmem_limit_bytes=VMEM_BYTES
        ),
        name="decode_step",
    )(
        lengths,
        queries,
        new_keys,
        new_values,
        residual,
        norm_gain.reshape(1, -1),
        targets.reshape(1, -1),
        old_sums.reshape(1, -1),
        rewards.reshape(1, -1),
        group_ids.reshape(1, -1),
        stored_keys,
        stored_values,
        out_proj,
        embedding,
    )
    return logprob.reshape(-1), advantage.reshape(-1)


def fits_one_kernel(tps, reps, stored_keys, out_proj, residual, embedding):
    samp, heads_kv, span, depth = stored_keys.shape
    total_samp = samp * reps
    return (
        span == 128
        and depth == 128
        and samp % 16 == 0
        and samp <= 128
        and reps % 2 == 0
        and total_samp == 128
        and total_samp % (16 * tps) == 0
        and 2 * out_proj.shape[1] % 128 == 0
        and embedding.shape[0] >= SLOTS * ROWS_PER_BLOCK
        and embedding.shape[0] % 16 == 0
        and embedding.shape[1] == reps * out_proj.shape[1]
    )


def per_device_best(*args):
    tps, reps = lax.axis_size("tp"), lax.axis_size("rep")
    if fits_one_kernel(tps, reps, args[3], args[6], args[7], args[9]):
        return one_kernel(*args)
    return per_device(*args)


def solution(mesh):
    in_specs = (
        P("rep", "tp"),
        P("rep", "tp"),
        P("rep", "tp"),
        P("rep", "tp", None, None),
        P("rep", "tp", None, None),
        P("rep"),
        P("tp", "rep"),
        P(None, "rep"),
        P(),
        P(("tp", "rep"), None),
        P(),
        P("rep"),
        P("rep"),
        P("rep"),
    )
    out_specs = (P("rep"), P("rep"))
    return jax.shard_map(
        per_device_best, mesh=mesh, in_specs=in_specs, out_specs=out_specs, check_vma=False
    )
```

```python
import functools

import jax
import jax.numpy as jnp
from jax import lax
from jax.experimental import pallas as pl
from jax.experimental.pallas import tpu as pltpu
from jax.sharding import PartitionSpec as P

MESH = pl.DeviceIdType.MESH
ROWS_PER_BLOCK = 512
SLOTS = 10
VMEM_BYTES = 66 * 1000 * 1000

GROUP = 8


def attention(queries, new_keys, new_values, stored_keys, stored_values, lengths):
    samp, heads_kv, span, depth = stored_keys.shape
    sample_ratio = queries.shape[1] // (heads_kv * depth)
    query_vector = queries.reshape(samp, heads_kv, sample_ratio, depth)
    scores = (
        jnp.einsum("sgqd,sgpd->sgqp", query_vector, stored_keys, preferred_element_type=jnp.float32)
        / 12.0
    )
    scores = 50.0 * jnp.tanh(scores / 50.0)
    valid = lax.broadcasted_iota(jnp.int32, (samp, 1, 1, span), 3) < lengths[:, None, None, None]
    expo = jnp.where(valid, jnp.exp(scores), 0.0)
    own_logit = (
        jnp.einsum(
            "sgqd,sgd->sgq",
            query_vector,
            new_keys.reshape(samp, heads_kv, depth),
            preferred_element_type=jnp.float32,
        )
        / 12.0
    )
    own_logit = 50.0 * jnp.tanh(own_logit / 50.0)
    own_exp = jnp.exp(own_logit)
    total = jnp.sum(expo, -1) + own_exp
    probs = (expo / total[..., None]).astype(jnp.bfloat16)
    own_probability = (own_exp / total).astype(jnp.bfloat16)
    attended_output = jnp.einsum(
        "sgqp,sgpd->sgqd", probs, stored_values, preferred_element_type=jnp.float32
    )
    attended_output = attended_output + own_probability.astype(jnp.float32)[
        ..., None
    ] * new_values.reshape(samp, heads_kv, 1, depth).astype(jnp.float32)
    return attended_output.reshape(samp, sample_ratio * heads_kv * depth).astype(jnp.bfloat16)


def per_device(
    queries,
    new_keys,
    new_values,
    stored_keys,
    stored_values,
    lengths,
    out_proj,
    residual,
    norm_gain,
    embedding,
    targets,
    old_sums,
    rewards,
    group_ids,
):
    samp = queries.shape[0]
    reps = lax.axis_size("rep")
    rep_index = lax.axis_index("rep")
    tp_index = lax.axis_index("tp")
    groups = samp * reps // GROUP
    member = group_ids[:, None] == lax.broadcasted_iota(jnp.int32, (1, groups), 1)
    reward_part = jnp.sum(jnp.where(member, rewards[:, None], 0.0), 0)
    group_total = lax.psum(reward_part, "rep")
    mine = jnp.sum(jnp.where(member, group_total[None, :], 0.0), 1)
    advantage = rewards - (mine - rewards) / (GROUP - 1.0)
    context = attention(queries, new_keys, new_values, stored_keys, stored_values, lengths)
    partial_value = jnp.dot(
        lax.all_gather(context, "rep", axis=0, tiled=True),
        out_proj,
        preferred_element_type=jnp.float32,
    )
    vocab_rows = embedding.shape[0]
    contract = (((1,), (1,)), ((), ()))
    heads = lax.psum(partial_value, "tp")
    stream = residual.astype(jnp.float32) + heads
    full = lax.all_gather(stream, "rep", axis=1, tiled=True)
    scale = lax.rsqrt(jnp.mean(full * full, axis=1, keepdims=True) + 1e-06)
    normed = (full * scale * norm_gain[None, :]).astype(jnp.bfloat16)
    logits = lax.dot_general(normed, embedding, contract, preferred_element_type=jnp.float32)
    capped = 30.0 * jnp.tanh(logits / 30.0)
    offset = (tp_index * reps + rep_index) * vocab_rows
    entry_ids = offset + lax.broadcasted_iota(jnp.int32, (1, vocab_rows), 1)
    picked_part = jnp.sum(jnp.where(entry_ids == targets[:, None], capped, 0.0), 1)
    total, picked = lax.psum((jnp.sum(jnp.exp(capped), 1), picked_part), ("tp", "rep"))
    logprob = picked - jnp.log(total)
    own_rows = lax.dynamic_slice_in_dim(logprob, rep_index * samp, samp)
    logprob_sum = old_sums + own_rows
    return (logprob_sum, advantage)


def as_column(row, count):
    eye = lax.broadcasted_iota(jnp.int32, (count, count), 0) == lax.broadcasted_iota(
        jnp.int32, (count, count), 1
    )
    return jnp.sum(jnp.where(eye, row, 0.0), 1, keepdims=True)


def as_row(column, count):
    eye = lax.broadcasted_iota(jnp.int32, (count, count), 0) == lax.broadcasted_iota(
        jnp.int32, (count, count), 1
    )
    return jnp.sum(jnp.where(eye, column, 0.0), 0, keepdims=True)


def step_kernel(
    tps,
    reps,
    lengths_hbm,
    queries_hbm,
    new_keys_hbm,
    new_values_hbm,
    residual_hbm,
    gain_hbm,
    targets_hbm,
    rewards_hbm,
    group_ids_hbm,
    keys_hbm,
    values_hbm,
    proj_hbm,
    table_hbm,
    out,
    lengths,
    queries,
    new_keys,
    new_values,
    residual,
    gain,
    targets,
    rewards,
    group_ids,
    keys,
    values,
    proj,
    table,
    raw,
    total_acc,
    picked_acc,
    q_rows,
    nk_rows,
    nv_rows,
    ctx_rows,
    context,
    partial,
    reduced,
    resid,
    blocks,
    normed,
    reward_rows,
    final_tp,
    final_rep,
    local_sem,
    table_sem,
    send_sem,
    ctx_sem,
    red_sem,
    block_sem,
    reward_sem,
    ftp_sem,
    frep_sem,
):
    t = lax.axis_index("tp")
    r = lax.axis_index("rep")
    samp, heads_kv, span, depth = keys_hbm.shape
    heads = queries.shape[1] // depth
    ratio = heads // heads_kv
    total_samp = samp * reps
    cols = residual.shape[0]
    padded = blocks.shape[2]
    share = total_samp // tps
    vocab_rows, width = table_hbm.shape
    full = vocab_rows // ROWS_PER_BLOCK
    tail = vocab_rows - full * ROWS_PER_BLOCK
    zs = reps // 2
    core = lax.rem(r, 2)
    partner = r + 1 - 2 * core
    sent = []

    def table_copy(index, slot):
        return pltpu.make_async_copy(
            table_hbm.at[pl.ds(pl.multiple_of(index * ROWS_PER_BLOCK, ROWS_PER_BLOCK), ROWS_PER_BLOCK)],
            table.at[slot],
            table_sem.at[slot],
        )

    def tail_copy():
        slot = full % SLOTS
        return pltpu.make_async_copy(
            table_hbm.at[pl.ds(full * ROWS_PER_BLOCK, tail)],
            table.at[slot, pl.ds(0, tail)],
            table_sem.at[slot],
        )

    moves = [
        (rewards_hbm, rewards),
        (group_ids_hbm, group_ids),
        (queries_hbm, queries),
        (new_keys_hbm, new_keys),
        (new_values_hbm, new_values),
        (lengths_hbm, lengths),
        (keys_hbm, keys),
        (values_hbm, values),
        (proj_hbm, proj),
        (residual_hbm, residual),
        (gain_hbm, gain),
        (targets_hbm, targets),
    ]
    copies = [
        pltpu.make_async_copy(src, dst, local_sem.at[n]) for n, (src, dst) in enumerate(moves)
    ]
    for copy in copies:
        copy.start()

    barrier = pltpu.get_barrier_semaphore()
    for k in range(1, tps):
        pl.semaphore_signal(
            barrier, inc=1, device_id=(lax.rem(t + k, tps), r), device_id_type=MESH
        )
    for k in range(1, reps):
        pl.semaphore_signal(
            barrier, inc=1, device_id=(t, lax.rem(r + k, reps)), device_id_type=MESH
        )

    def send(src, dst, recv, device):
        copy = pltpu.make_async_remote_copy(
            src_ref=src,
            dst_ref=dst,
            send_sem=send_sem.at[len(sent)],
            recv_sem=recv,
            device_id=device,
            device_id_type=MESH,
        )
        copy.start()
        sent.append(copy)

    def received(ref, recv):
        pltpu.make_async_remote_copy(
            src_ref=ref,
            dst_ref=ref,
            send_sem=send_sem.at[0],
            recv_sem=recv,
            device_id=(t, partner),
            device_id_type=MESH,
        ).wait_recv()

    for copy in copies[0:6]:
        copy.wait()
    reward_rows[r] = jnp.zeros(reward_rows.shape[1:], jnp.float32)
    reward_rows[r, 0:1, 0:samp] = rewards[...]
    reward_rows[r, 1:2, 0:samp] = group_ids[...].astype(jnp.float32)

    for h in range(heads):
        g = h // ratio
        q_rows[:, h, :] = queries[:, h * depth : (h + 1) * depth].astype(jnp.float32)
        nk_rows[:, h, :] = new_keys[:, g * depth : (g + 1) * depth].astype(jnp.float32)
        nv_rows[:, h, :] = new_values[:, g * depth : (g + 1) * depth].astype(jnp.float32)

    head_group = lax.broadcasted_iota(jnp.int32, (heads, span), 0) // ratio
    position = lax.broadcasted_iota(jnp.int32, (heads, span), 1)
    copies[6].wait()
    for index in range(SLOTS):
        table_copy(index, index).start()
    probs = []
    own_probs = []
    for s in range(samp):
        query = q_rows[s]
        wide = lax.dot_general(
            query.astype(jnp.bfloat16),
            keys[s].reshape(heads_kv * span, depth),
            (((1,), (1,)), ((), ())),
            preferred_element_type=jnp.float32,
        )
        scores = wide[:, 0:span]
        for g in range(1, heads_kv):
            scores = jnp.where(head_group == g, wide[:, g * span : (g + 1) * span], scores)
        scores = 50.0 * jnp.tanh(scores / 12.0 / 50.0)
        expo = jnp.where(position < lengths[s], jnp.exp(scores), 0.0)
        own = jnp.sum(query * nk_rows[s], 1, keepdims=True) / 12.0
        own_exp = jnp.exp(50.0 * jnp.tanh(own / 50.0))
        total = jnp.sum(expo, 1, keepdims=True) + own_exp
        probs.append((expo / total).astype(jnp.bfloat16).astype(jnp.float32))
        own_probs.append((own_exp / total).astype(jnp.bfloat16).astype(jnp.float32))
    copies[7].wait()
    for s in range(samp):
        spread = jnp.concatenate(
            [jnp.where(head_group == g, probs[s], 0.0) for g in range(heads_kv)], axis=1
        )
        attended = jnp.dot(
            spread.astype(jnp.bfloat16),
            values[s].reshape(heads_kv * span, depth),
            preferred_element_type=jnp.float32,
        )
        ctx_rows[s] = attended + own_probs[s] * nv_rows[s]
    own_ctx = context.at[pl.ds(pl.multiple_of(r * samp, samp), samp)]
    for h in range(heads):
        own_ctx[:, h * depth : (h + 1) * depth] = ctx_rows[:, h, :].astype(jnp.bfloat16)

    pl.semaphore_wait(barrier, tps + reps - 2)

    def ctx_slot(q):
        return context.at[pl.ds(pl.multiple_of(q * samp, samp), samp)]

    for k in range(1, zs):
        send(ctx_slot(r), ctx_slot(r), ctx_sem.at[r], (t, lax.rem(r + 2 * k, reps)))
    send(ctx_slot(r), ctx_slot(r), ctx_sem.at[r], (t, partner))
    for k in range(1, reps):
        send(reward_rows.at[r], reward_rows.at[r], reward_sem.at[r], (t, lax.rem(r + k, reps)))
    for k in range(1, zs):
        q = lax.rem(r + 2 * k, reps)
        received(ctx_slot(q), ctx_sem.at[q])
        send(ctx_slot(q), ctx_slot(q), ctx_sem.at[q], (t, partner))
    for k in range(zs):
        q = lax.rem(partner + 2 * k, reps)
        received(ctx_slot(q), ctx_sem.at[q])

    for copy in copies[8:]:
        copy.wait()
    product = lax.dot_general(
        context[...], proj[...], (((1,), (1,)), ((), ())), preferred_element_type=jnp.float32
    )
    for k in range(tps):
        partial[k] = product[k * share : (k + 1) * share]
    for k in range(1, tps):
        u = lax.rem(t + k, tps)
        send(partial.at[u], reduced.at[t], red_sem.at[t], (u, r))
    reduced[t] = partial[t]
    gain_row = jnp.concatenate([gain[n : n + 1] for n in range(gain.shape[0])], axis=1)
    own_gain = gain_row[:, 0:cols]
    for q in range(1, reps):
        own_gain = jnp.where(r == q, gain_row[:, q * cols : (q + 1) * cols], own_gain)
    turned = jnp.transpose(residual[...].astype(jnp.float32))
    for k in range(tps):
        resid[k] = turned[k * share : (k + 1) * share]
    rest = resid[t]
    for k in range(1, tps):
        u = lax.rem(t + k, tps)
        received(reduced.at[u], red_sem.at[u])
    stream = reduced[0]
    for k in range(1, tps):
        stream = stream + reduced[k]
    stream = stream + rest
    square = jnp.sum(stream * stream, 1, keepdims=True)
    high = square.astype(jnp.bfloat16).astype(jnp.float32)
    mid = (square - high).astype(jnp.bfloat16).astype(jnp.float32)
    low = square - high - mid
    lane = lax.broadcasted_iota(jnp.int32, (share, padded - cols), 1)
    extra = jnp.where(lane == 0, high, jnp.where(lane == 1, mid, jnp.where(lane == 2, low, 0.0)))
    mine = blocks.at[r, pl.ds(pl.multiple_of(t * share, share), share)]
    mine[:, 0:cols] = (stream * own_gain).astype(jnp.bfloat16)
    mine[:, cols:padded] = extra.astype(jnp.bfloat16)

    def block(u, q):
        return blocks.at[q, pl.ds(pl.multiple_of(u * share, share), share)]

    def arrived(u, q):
        return block_sem.at[u * reps + q]

    for k in range(1, zs):
        send(block(t, r), block(t, r), arrived(t, r), (t, lax.rem(r + 2 * k, reps)))
    for step in range(zs):
        q = lax.rem(r + 2 * step, reps)
        if step:
            received(block(t, q), arrived(t, q))
        for k in range(1, tps):
            send(block(t, q), block(t, q), arrived(t, q), (lax.rem(t + k, tps), r))
        send(block(t, q), block(t, q), arrived(t, q), (t, partner))
    for step in range(zs):
        q = lax.rem(r + 2 * step, reps)
        for k in range(1, tps):
            u = lax.rem(t + k, tps)
            received(block(u, q), arrived(u, q))
            send(block(u, q), block(u, q), arrived(u, q), (t, partner))
    for step in range(zs):
        q = lax.rem(partner + 2 * step, reps)
        for k in range(tps):
            u = lax.rem(t + k, tps)
            received(block(u, q), arrived(u, q))

    squares = jnp.zeros((total_samp, 1), jnp.float32)
    for z in range(zs):
        left = blocks[2 * z].astype(jnp.float32)
        right = blocks[2 * z + 1].astype(jnp.float32)
        pair = jnp.concatenate([left[:, 0:cols], right[:, 0:cols]], axis=1)
        normed[:, 2 * z * cols : 2 * (z + 1) * cols] = pair.astype(jnp.bfloat16)
        squares = squares + jnp.sum(left[:, cols:padded], 1, keepdims=True)
        squares = squares + jnp.sum(right[:, cols:padded], 1, keepdims=True)
    scale = lax.rsqrt(squares / width + 1e-06) / 30.0
    wanted = as_column(targets[...].astype(jnp.float32), total_samp).astype(jnp.int32)
    wanted = wanted - (t * reps + r) * vocab_rows

    def product_of(rows, half):
        raw[half, :, 0 : rows.shape[0]] = lax.dot_general(
            normed[...], rows, (((1,), (1,)), ((), ())), preferred_element_type=jnp.float32
        )

    def score(half, count, first):
        for low in range(0, count, 128):
            lanes = min(128, count - low)
            capped = 30.0 * jnp.tanh(raw[half, :, low : low + lanes] * scale)
            entry = lax.broadcasted_iota(jnp.int32, capped.shape, 1) + (first + low)
            total_acc[:, 0:lanes] += jnp.exp(capped)
            picked_acc[:, 0:lanes] += jnp.where(entry == wanted, capped, 0.0)

    def refill(index, slot):
        @pl.when(index + SLOTS < full)
        def _():
            table_copy(index + SLOTS, slot).start()

        if tail:

            @pl.when(index + SLOTS == full)
            def _():
                tail_copy().start()

    total_acc[...] = jnp.zeros_like(total_acc)
    picked_acc[...] = jnp.zeros_like(picked_acc)
    table_copy(0, 0).wait()
    product_of(table[0], 0)
    refill(0, 0)

    def visit(pair, nothing):
        for half in (1, 0):
            index = 2 * pair + (1 if half else 2)
            slot = lax.rem(index, SLOTS)
            table_copy(index, slot).wait()
            product_of(table[slot], half)
            score(1 - half, ROWS_PER_BLOCK, (index - 1) * ROWS_PER_BLOCK)
            refill(index, slot)
        return nothing

    lax.fori_loop(0, (full - 1) // 2, visit, 0)
    if tail:
        tail_copy().wait()
        product_of(table[full % SLOTS, 0:tail], 1)
    score(0, ROWS_PER_BLOCK, (full - 1) * ROWS_PER_BLOCK)
    if tail:
        score(1, tail, full * ROWS_PER_BLOCK)
    carry = (
        jnp.sum(total_acc[...], 1, keepdims=True),
        jnp.sum(picked_acc[...], 1, keepdims=True),
    )

    final_tp[t] = jnp.zeros(final_tp.shape[1:], jnp.float32)
    final_tp[t, 0:1] = as_row(carry[0], total_samp)
    final_tp[t, 1:2] = as_row(carry[1], total_samp)
    for k in range(1, tps):
        send(final_tp.at[t], final_tp.at[t], ftp_sem.at[t], (lax.rem(t + k, tps), r))

    for k in range(1, reps):
        q = lax.rem(r + k, reps)
        received(reward_rows.at[q], reward_sem.at[q])
    own_ids = as_column(group_ids[...].astype(jnp.float32), samp)
    group_sum = jnp.zeros((samp, 1), jnp.float32)
    for q in range(reps):
        same = own_ids == reward_rows[q, 1:2, 0:samp]
        group_sum = group_sum + jnp.sum(
            jnp.where(same, reward_rows[q, 0:1, 0:samp], 0.0), 1, keepdims=True
        )
    out[1:2] = as_row(group_sum, samp)

    for k in range(1, tps):
        u = lax.rem(t + k, tps)
        received(final_tp.at[u], ftp_sem.at[u])
    column = final_tp[0]
    for k in range(1, tps):
        column = column + final_tp[k]
    final_rep[r] = column
    for k in range(1, reps):
        send(final_rep.at[r], final_rep.at[r], frep_sem.at[r], (t, lax.rem(r + k, reps)))
    for k in range(1, reps):
        q = lax.rem(r + k, reps)
        received(final_rep.at[q], frep_sem.at[q])
    whole = final_rep[0]
    for k in range(1, reps):
        whole = whole + final_rep[k]
    logprob = whole[1:2] - jnp.log(whole[0:1])
    chosen = lax.broadcasted_iota(jnp.int32, (samp, total_samp), 1) == (
        lax.broadcasted_iota(jnp.int32, (samp, total_samp), 0) + r * samp
    )
    own_rows = jnp.sum(jnp.where(chosen, logprob, 0.0), 1, keepdims=True)
    out[0:1] = as_row(own_rows, samp)
    for copy in sent:
        copy.wait_send()


def one_kernel(
    queries,
    new_keys,
    new_values,
    stored_keys,
    stored_values,
    lengths,
    out_proj,
    residual,
    norm_gain,
    embedding,
    targets,
    old_sums,
    rewards,
    group_ids,
):
    tps, reps = lax.axis_size("tp"), lax.axis_size("rep")
    samp, heads_kv, span, depth = stored_keys.shape
    heads = queries.shape[1] // depth
    total_samp = samp * reps
    cols = out_proj.shape[1]
    padded = (cols + 3 + 127) // 128 * 128
    share = total_samp // tps
    zs = reps // 2
    sends = (
        (zs - 1) + zs + (reps - 1) + (tps - 1) + (zs - 1) + zs * (tps - 1) + zs * tps
        + (tps - 1) + (reps - 1)
    )
    vmem = pl.BlockSpec(memory_space=pltpu.VMEM)
    hbm = pl.BlockSpec(memory_space=pltpu.HBM)
    dma = pltpu.SemaphoreType.DMA
    lanes_gain = norm_gain.reshape(-1, 128)
    sums = pl.pallas_call(
        functools.partial(step_kernel, tps, reps),
        out_shape=jax.ShapeDtypeStruct((2, samp), jnp.float32),
        in_specs=[hbm] * 13,
        out_specs=vmem,
        scratch_shapes=[
            pltpu.SMEM((samp,), jnp.int32),
            pltpu.VMEM(queries.shape, queries.dtype),
            pltpu.VMEM(new_keys.shape, new_keys.dtype),
            pltpu.VMEM(new_values.shape, new_values.dtype),
            pltpu.VMEM(residual.shape[::-1], residual.dtype),
            pltpu.VMEM(lanes_gain.shape, jnp.float32),
            pltpu.VMEM((1, total_samp), jnp.int32),
            pltpu.VMEM((1, samp), jnp.float32),
            pltpu.VMEM((1, samp), jnp.int32),
            pltpu.VMEM(stored_keys.shape, stored_keys.dtype),
            pltpu.VMEM(stored_values.shape, stored_values.dtype),
            pltpu.VMEM(out_proj.shape[::-1], out_proj.dtype),
            pltpu.VMEM((SLOTS, ROWS_PER_BLOCK, embedding.shape[1]), embedding.dtype),
            pltpu.VMEM((2, total_samp, ROWS_PER_BLOCK), jnp.float32),
            pltpu.VMEM((total_samp, 128), jnp.float32),
            pltpu.VMEM((total_samp, 128), jnp.float32),
            pltpu.VMEM((samp, heads, depth), jnp.float32),
            pltpu.VMEM((samp, heads, depth), jnp.float32),
            pltpu.VMEM((samp, heads, depth), jnp.float32),
            pltpu.VMEM((samp, heads, depth), jnp.float32),
            pltpu.VMEM((total_samp, heads * depth), jnp.bfloat16),
            pltpu.VMEM((tps, share, cols), jnp.float32),
            pltpu.VMEM((tps, share, cols), jnp.float32),
            pltpu.VMEM((tps, share, cols), jnp.float32),
            pltpu.VMEM((reps, total_samp, padded), jnp.bfloat16),
            pltpu.VMEM((total_samp, embedding.shape[1]), jnp.bfloat16),
            pltpu.VMEM((reps, 8, 128), jnp.float32),
            pltpu.VMEM((tps, 8, total_samp), jnp.float32),
            pltpu.VMEM((reps, 8, total_samp), jnp.float32),
            dma((12,)),
            dma((SLOTS,)),
            dma((sends,)),
            dma((reps,)),
            dma((tps,)),
            dma((tps * reps,)),
            dma((reps,)),
            dma((tps,)),
            dma((reps,)),
        ],
        compiler_params=pltpu.CompilerParams(
            collective_id=0, has_side_effects=True, vmem_limit_bytes=VMEM_BYTES
        ),
        name="decode_step",
    )(
        lengths,
        queries,
        new_keys,
        new_values,
        residual.T,
        lanes_gain,
        targets.reshape(1, -1),
        rewards.reshape(1, -1),
        group_ids.reshape(1, -1),
        stored_keys,
        stored_values,
        out_proj.T,
        embedding,
    )
    return old_sums + sums[0], rewards - (sums[1] - rewards) / (GROUP - 1.0)


def fits_one_kernel(tps, reps, stored_keys, out_proj, residual, embedding):
    samp, heads_kv, span, depth = stored_keys.shape
    total_samp = samp * reps
    return (
        span == 128
        and depth == 128
        and samp % 16 == 0
        and samp <= 128
        and reps % 2 == 0
        and total_samp == 128
        and total_samp % (16 * tps) == 0
        and 2 * out_proj.shape[1] % 128 == 0
        and out_proj.shape[1] % 16 == 0
        and embedding.shape[0] >= SLOTS * ROWS_PER_BLOCK
        and embedding.shape[0] % 16 == 0
        and embedding.shape[0] // ROWS_PER_BLOCK % 2 == 1
        and embedding.shape[1] == reps * out_proj.shape[1]
    )


def per_device_best(*args):
    tps, reps = lax.axis_size("tp"), lax.axis_size("rep")
    if fits_one_kernel(tps, reps, args[3], args[6], args[7], args[9]):
        return one_kernel(*args)
    return per_device(*args)


def solution(mesh):
    in_specs = (
        P("rep", "tp"),
        P("rep", "tp"),
        P("rep", "tp"),
        P("rep", "tp", None, None),
        P("rep", "tp", None, None),
        P("rep"),
        P("tp", "rep"),
        P(None, "rep"),
        P(),
        P(("tp", "rep"), None),
        P(),
        P("rep"),
        P("rep"),
        P("rep"),
    )
    out_specs = (P("rep"), P("rep"))
    return jax.shard_map(
        per_device_best, mesh=mesh, in_specs=in_specs, out_specs=out_specs, check_vma=False
    )
```

```python
import functools

import jax
import jax.numpy as jnp
from jax import lax
from jax.experimental import pallas as pl
from jax.experimental.pallas import tpu as pltpu
from jax.sharding import PartitionSpec as P

MESH = pl.DeviceIdType.MESH
ROWS_PER_BLOCK = 512
SLOTS = 10
VMEM_BYTES = 66 * 1000 * 1000

GROUP = 8


def attention(queries, new_keys, new_values, stored_keys, stored_values, lengths):
    samp, heads_kv, span, depth = stored_keys.shape
    sample_ratio = queries.shape[1] // (heads_kv * depth)
    query_vector = queries.reshape(samp, heads_kv, sample_ratio, depth)
    scores = (
        jnp.einsum("sgqd,sgpd->sgqp", query_vector, stored_keys, preferred_element_type=jnp.float32)
        / 12.0
    )
    scores = 50.0 * jnp.tanh(scores / 50.0)
    valid = lax.broadcasted_iota(jnp.int32, (samp, 1, 1, span), 3) < lengths[:, None, None, None]
    expo = jnp.where(valid, jnp.exp(scores), 0.0)
    own_logit = (
        jnp.einsum(
            "sgqd,sgd->sgq",
            query_vector,
            new_keys.reshape(samp, heads_kv, depth),
            preferred_element_type=jnp.float32,
        )
        / 12.0
    )
    own_logit = 50.0 * jnp.tanh(own_logit / 50.0)
    own_exp = jnp.exp(own_logit)
    total = jnp.sum(expo, -1) + own_exp
    probs = (expo / total[..., None]).astype(jnp.bfloat16)
    own_probability = (own_exp / total).astype(jnp.bfloat16)
    attended_output = jnp.einsum(
        "sgqp,sgpd->sgqd", probs, stored_values, preferred_element_type=jnp.float32
    )
    attended_output = attended_output + own_probability.astype(jnp.float32)[
        ..., None
    ] * new_values.reshape(samp, heads_kv, 1, depth).astype(jnp.float32)
    return attended_output.reshape(samp, sample_ratio * heads_kv * depth).astype(jnp.bfloat16)


def per_device(
    queries,
    new_keys,
    new_values,
    stored_keys,
    stored_values,
    lengths,
    out_proj,
    residual,
    norm_gain,
    embedding,
    targets,
    old_sums,
    rewards,
    group_ids,
):
    samp = queries.shape[0]
    reps = lax.axis_size("rep")
    rep_index = lax.axis_index("rep")
    tp_index = lax.axis_index("tp")
    groups = samp * reps // GROUP
    member = group_ids[:, None] == lax.broadcasted_iota(jnp.int32, (1, groups), 1)
    reward_part = jnp.sum(jnp.where(member, rewards[:, None], 0.0), 0)
    group_total = lax.psum(reward_part, "rep")
    mine = jnp.sum(jnp.where(member, group_total[None, :], 0.0), 1)
    advantage = rewards - (mine - rewards) / (GROUP - 1.0)
    context = attention(queries, new_keys, new_values, stored_keys, stored_values, lengths)
    partial_value = jnp.dot(
        lax.all_gather(context, "rep", axis=0, tiled=True),
        out_proj,
        preferred_element_type=jnp.float32,
    )
    vocab_rows = embedding.shape[0]
    contract = (((1,), (1,)), ((), ()))
    heads = lax.psum(partial_value, "tp")
    stream = residual.astype(jnp.float32) + heads
    full = lax.all_gather(stream, "rep", axis=1, tiled=True)
    scale = lax.rsqrt(jnp.mean(full * full, axis=1, keepdims=True) + 1e-06)
    normed = (full * scale * norm_gain[None, :]).astype(jnp.bfloat16)
    logits = lax.dot_general(normed, embedding, contract, preferred_element_type=jnp.float32)
    capped = 30.0 * jnp.tanh(logits / 30.0)
    offset = (tp_index * reps + rep_index) * vocab_rows
    entry_ids = offset + lax.broadcasted_iota(jnp.int32, (1, vocab_rows), 1)
    picked_part = jnp.sum(jnp.where(entry_ids == targets[:, None], capped, 0.0), 1)
    total, picked = lax.psum((jnp.sum(jnp.exp(capped), 1), picked_part), ("tp", "rep"))
    logprob = picked - jnp.log(total)
    own_rows = lax.dynamic_slice_in_dim(logprob, rep_index * samp, samp)
    logprob_sum = old_sums + own_rows
    return (logprob_sum, advantage)


def as_column(row, count):
    eye = lax.broadcasted_iota(jnp.int32, (count, count), 0) == lax.broadcasted_iota(
        jnp.int32, (count, count), 1
    )
    return jnp.sum(jnp.where(eye, row, 0.0), 1, keepdims=True)


def as_row(column, count):
    eye = lax.broadcasted_iota(jnp.int32, (count, count), 0) == lax.broadcasted_iota(
        jnp.int32, (count, count), 1
    )
    return jnp.sum(jnp.where(eye, column, 0.0), 0, keepdims=True)


def step_kernel(
    tps,
    reps,
    lengths_hbm,
    queries_hbm,
    new_keys_hbm,
    new_values_hbm,
    residual_hbm,
    gain_hbm,
    targets_hbm,
    rewards_hbm,
    group_ids_hbm,
    keys_hbm,
    values_hbm,
    proj_hbm,
    table_hbm,
    out,
    lengths,
    queries,
    new_keys,
    new_values,
    residual,
    gain,
    targets,
    rewards,
    group_ids,
    keys,
    values,
    proj,
    table,
    raw,
    total_acc,
    picked_acc,
    q_rows,
    nk_rows,
    nv_rows,
    ctx_rows,
    context,
    partial,
    reduced,
    resid,
    blocks,
    normed,
    reward_rows,
    final_tp,
    final_rep,
    local_sem,
    table_sem,
    send_sem,
    ctx_sem,
    red_sem,
    block_sem,
    reward_sem,
    ftp_sem,
    frep_sem,
):
    t = lax.axis_index("tp")
    r = lax.axis_index("rep")
    samp, heads_kv, span, depth = keys_hbm.shape
    heads = queries.shape[1] // depth
    ratio = heads // heads_kv
    total_samp = samp * reps
    cols = residual.shape[0]
    padded = blocks.shape[2]
    share = total_samp // tps
    vocab_rows, width = table_hbm.shape
    full = vocab_rows // ROWS_PER_BLOCK
    tail = vocab_rows - full * ROWS_PER_BLOCK
    zs = reps // 2
    core = lax.rem(r, 2)
    partner = r + 1 - 2 * core
    sent = []

    def table_copy(index, slot):
        return pltpu.make_async_copy(
            table_hbm.at[pl.ds(pl.multiple_of(index * ROWS_PER_BLOCK, ROWS_PER_BLOCK), ROWS_PER_BLOCK)],
            table.at[slot],
            table_sem.at[slot],
        )

    def tail_copy():
        slot = full % SLOTS
        return pltpu.make_async_copy(
            table_hbm.at[pl.ds(full * ROWS_PER_BLOCK, tail)],
            table.at[slot, pl.ds(0, tail)],
            table_sem.at[slot],
        )

    moves = [
        (rewards_hbm, rewards),
        (group_ids_hbm, group_ids),
        (queries_hbm, queries),
        (new_keys_hbm, new_keys),
        (new_values_hbm, new_values),
        (lengths_hbm, lengths),
        (keys_hbm, keys),
        (values_hbm, values),
        (proj_hbm, proj),
        (residual_hbm, residual),
        (gain_hbm, gain),
        (targets_hbm, targets),
    ]
    copies = [
        pltpu.make_async_copy(src, dst, local_sem.at[n]) for n, (src, dst) in enumerate(moves)
    ]
    for copy in copies:
        copy.start()

    barrier = pltpu.get_barrier_semaphore()
    for k in range(1, tps):
        pl.semaphore_signal(
            barrier, inc=1, device_id=(lax.rem(t + k, tps), r), device_id_type=MESH
        )
    for k in range(1, reps):
        pl.semaphore_signal(
            barrier, inc=1, device_id=(t, lax.rem(r + k, reps)), device_id_type=MESH
        )

    def send(src, dst, recv, device):
        copy = pltpu.make_async_remote_copy(
            src_ref=src,
            dst_ref=dst,
            send_sem=send_sem.at[len(sent)],
            recv_sem=recv,
            device_id=device,
            device_id_type=MESH,
        )
        copy.start()
        sent.append(copy)

    def received(ref, recv):
        pltpu.make_async_remote_copy(
            src_ref=ref,
            dst_ref=ref,
            send_sem=send_sem.at[0],
            recv_sem=recv,
            device_id=(t, partner),
            device_id_type=MESH,
        ).wait_recv()

    for copy in copies[0:6]:
        copy.wait()
    reward_rows[r] = jnp.zeros(reward_rows.shape[1:], jnp.float32)
    reward_rows[r, 0:1, 0:samp] = rewards[...]
    reward_rows[r, 1:2, 0:samp] = group_ids[...].astype(jnp.float32)

    for h in range(heads):
        g = h // ratio
        q_rows[:, h, :] = queries[:, h * depth : (h + 1) * depth].astype(jnp.float32)
        nk_rows[:, h, :] = new_keys[:, g * depth : (g + 1) * depth].astype(jnp.float32)
        nv_rows[:, h, :] = new_values[:, g * depth : (g + 1) * depth].astype(jnp.float32)

    head_group = lax.broadcasted_iota(jnp.int32, (heads, span), 0) // ratio
    position = lax.broadcasted_iota(jnp.int32, (heads, span), 1)
    copies[6].wait()
    for index in range(SLOTS):
        table_copy(index, index).start()
    probs = []
    own_probs = []
    for s in range(samp):
        query = q_rows[s]
        wide = lax.dot_general(
            query.astype(jnp.bfloat16),
            keys[s].reshape(heads_kv * span, depth),
            (((1,), (1,)), ((), ())),
            preferred_element_type=jnp.float32,
        )
        scores = wide[:, 0:span]
        for g in range(1, heads_kv):
            scores = jnp.where(head_group == g, wide[:, g * span : (g + 1) * span], scores)
        scores = 50.0 * jnp.tanh(scores / 12.0 / 50.0)
        expo = jnp.where(position < lengths[s], jnp.exp(scores), 0.0)
        own = jnp.sum(query * nk_rows[s], 1, keepdims=True) / 12.0
        own_exp = jnp.exp(50.0 * jnp.tanh(own / 50.0))
        total = jnp.sum(expo, 1, keepdims=True) + own_exp
        probs.append((expo / total).astype(jnp.bfloat16).astype(jnp.float32))
        own_probs.append((own_exp / total).astype(jnp.bfloat16).astype(jnp.float32))
    copies[7].wait()
    for s in range(samp):
        spread = jnp.concatenate(
            [jnp.where(head_group == g, probs[s], 0.0) for g in range(heads_kv)], axis=1
        )
        attended = jnp.dot(
            spread.astype(jnp.bfloat16),
            values[s].reshape(heads_kv * span, depth),
            preferred_element_type=jnp.float32,
        )
        ctx_rows[s] = attended + own_probs[s] * nv_rows[s]
    own_ctx = context.at[pl.ds(pl.multiple_of(r * samp, samp), samp)]
    for h in range(heads):
        own_ctx[:, h * depth : (h + 1) * depth] = ctx_rows[:, h, :].astype(jnp.bfloat16)

    pl.semaphore_wait(barrier, tps + reps - 2)

    def ctx_slot(q):
        return context.at[pl.ds(pl.multiple_of(q * samp, samp), samp)]

    for k in range(1, zs):
        send(ctx_slot(r), ctx_slot(r), ctx_sem.at[r], (t, lax.rem(r + 2 * k, reps)))
    send(ctx_slot(r), ctx_slot(r), ctx_sem.at[r], (t, partner))
    for k in range(1, reps):
        send(reward_rows.at[r], reward_rows.at[r], reward_sem.at[r], (t, lax.rem(r + k, reps)))
    for k in range(1, zs):
        q = lax.rem(r + 2 * k, reps)
        received(ctx_slot(q), ctx_sem.at[q])
        send(ctx_slot(q), ctx_slot(q), ctx_sem.at[q], (t, partner))
    for k in range(zs):
        q = lax.rem(partner + 2 * k, reps)
        received(ctx_slot(q), ctx_sem.at[q])

    for copy in copies[8:]:
        copy.wait()
    product = lax.dot_general(
        context[...], proj[...], (((1,), (1,)), ((), ())), preferred_element_type=jnp.float32
    )
    for k in range(tps):
        partial[k] = product[k * share : (k + 1) * share].astype(jnp.bfloat16)
    for k in range(1, tps):
        u = lax.rem(t + k, tps)
        send(partial.at[u], reduced.at[t], red_sem.at[t], (u, r))
    gain_row = jnp.concatenate([gain[n : n + 1] for n in range(gain.shape[0])], axis=1)
    own_gain = gain_row[:, 0:cols]
    for q in range(1, reps):
        own_gain = jnp.where(r == q, gain_row[:, q * cols : (q + 1) * cols], own_gain)
    turned = jnp.transpose(residual[...].astype(jnp.float32))
    for k in range(tps):
        rows = slice(k * share, (k + 1) * share)
        resid[k] = turned[rows] + product[rows]
    rest = resid[t]
    for k in range(1, tps):
        u = lax.rem(t + k, tps)
        received(reduced.at[u], red_sem.at[u])
    stream = rest
    for k in range(1, tps):
        stream = stream + reduced[lax.rem(t + k, tps)].astype(jnp.float32)
    square = jnp.sum(stream * stream, 1, keepdims=True)
    high = square.astype(jnp.bfloat16).astype(jnp.float32)
    mid = (square - high).astype(jnp.bfloat16).astype(jnp.float32)
    low = square - high - mid
    lane = lax.broadcasted_iota(jnp.int32, (share, padded - cols), 1)
    extra = jnp.where(lane == 0, high, jnp.where(lane == 1, mid, jnp.where(lane == 2, low, 0.0)))
    mine = blocks.at[r, pl.ds(pl.multiple_of(t * share, share), share)]
    mine[:, 0:cols] = (stream * own_gain).astype(jnp.bfloat16)
    mine[:, cols:padded] = extra.astype(jnp.bfloat16)

    def block(u, q):
        return blocks.at[q, pl.ds(pl.multiple_of(u * share, share), share)]

    def arrived(u, q):
        return block_sem.at[u * reps + q]

    for k in range(1, zs):
        send(block(t, r), block(t, r), arrived(t, r), (t, lax.rem(r + 2 * k, reps)))
    for step in range(zs):
        q = lax.rem(r + 2 * step, reps)
        if step:
            received(block(t, q), arrived(t, q))
        for k in range(1, tps):
            send(block(t, q), block(t, q), arrived(t, q), (lax.rem(t + k, tps), r))
        send(block(t, q), block(t, q), arrived(t, q), (t, partner))
    for step in range(zs):
        q = lax.rem(r + 2 * step, reps)
        for k in range(1, tps):
            u = lax.rem(t + k, tps)
            received(block(u, q), arrived(u, q))
            send(block(u, q), block(u, q), arrived(u, q), (t, partner))
    for step in range(zs):
        q = lax.rem(partner + 2 * step, reps)
        for k in range(tps):
            u = lax.rem(t + k, tps)
            received(block(u, q), arrived(u, q))

    squares = jnp.zeros((total_samp, 1), jnp.float32)
    for z in range(zs):
        left = blocks[2 * z].astype(jnp.float32)
        right = blocks[2 * z + 1].astype(jnp.float32)
        pair = jnp.concatenate([left[:, 0:cols], right[:, 0:cols]], axis=1)
        normed[:, 2 * z * cols : 2 * (z + 1) * cols] = pair.astype(jnp.bfloat16)
        squares = squares + jnp.sum(left[:, cols:padded], 1, keepdims=True)
        squares = squares + jnp.sum(right[:, cols:padded], 1, keepdims=True)
    scale = lax.rsqrt(squares / width + 1e-06) / 30.0
    wanted = as_column(targets[...].astype(jnp.float32), total_samp).astype(jnp.int32)
    wanted = wanted - (t * reps + r) * vocab_rows

    def product_of(rows, half):
        raw[half, :, 0 : rows.shape[0]] = lax.dot_general(
            normed[...], rows, (((1,), (1,)), ((), ())), preferred_element_type=jnp.float32
        )

    def score(half, count, first):
        for low in range(0, count, 128):
            lanes = min(128, count - low)
            capped = 30.0 * jnp.tanh(raw[half, :, low : low + lanes] * scale)
            entry = lax.broadcasted_iota(jnp.int32, capped.shape, 1) + (first + low)
            total_acc[:, 0:lanes] += jnp.exp(capped)
            picked_acc[:, 0:lanes] += jnp.where(entry == wanted, capped, 0.0)

    def refill(index, slot):
        @pl.when(index + SLOTS < full)
        def _():
            table_copy(index + SLOTS, slot).start()

        if tail:

            @pl.when(index + SLOTS == full)
            def _():
                tail_copy().start()

    total_acc[...] = jnp.zeros_like(total_acc)
    picked_acc[...] = jnp.zeros_like(picked_acc)
    table_copy(0, 0).wait()
    product_of(table[0], 0)
    refill(0, 0)

    def visit(pair, nothing):
        for half in (1, 0):
            index = 2 * pair + (1 if half else 2)
            slot = lax.rem(index, SLOTS)
            table_copy(index, slot).wait()
            product_of(table[slot], half)
            score(1 - half, ROWS_PER_BLOCK, (index - 1) * ROWS_PER_BLOCK)
            refill(index, slot)
        return nothing

    lax.fori_loop(0, (full - 1) // 2, visit, 0)
    if tail:
        tail_copy().wait()
        product_of(table[full % SLOTS, 0:tail], 1)
    score(0, ROWS_PER_BLOCK, (full - 1) * ROWS_PER_BLOCK)
    if tail:
        score(1, tail, full * ROWS_PER_BLOCK)
    carry = (
        jnp.sum(total_acc[...], 1, keepdims=True),
        jnp.sum(picked_acc[...], 1, keepdims=True),
    )

    final_tp[t] = jnp.zeros(final_tp.shape[1:], jnp.float32)
    final_tp[t, 0:1] = as_row(carry[0], total_samp)
    final_tp[t, 1:2] = as_row(carry[1], total_samp)
    for k in range(1, tps):
        send(final_tp.at[t], final_tp.at[t], ftp_sem.at[t], (lax.rem(t + k, tps), r))

    for k in range(1, reps):
        q = lax.rem(r + k, reps)
        received(reward_rows.at[q], reward_sem.at[q])
    own_ids = as_column(group_ids[...].astype(jnp.float32), samp)
    group_sum = jnp.zeros((samp, 1), jnp.float32)
    for q in range(reps):
        same = own_ids == reward_rows[q, 1:2, 0:samp]
        group_sum = group_sum + jnp.sum(
            jnp.where(same, reward_rows[q, 0:1, 0:samp], 0.0), 1, keepdims=True
        )
    out[1:2] = as_row(group_sum, samp)

    for k in range(1, tps):
        u = lax.rem(t + k, tps)
        received(final_tp.at[u], ftp_sem.at[u])
    column = final_tp[0]
    for k in range(1, tps):
        column = column + final_tp[k]
    final_rep[r] = column
    for k in range(1, reps):
        send(final_rep.at[r], final_rep.at[r], frep_sem.at[r], (t, lax.rem(r + k, reps)))
    for k in range(1, reps):
        q = lax.rem(r + k, reps)
        received(final_rep.at[q], frep_sem.at[q])
    whole = final_rep[0]
    for k in range(1, reps):
        whole = whole + final_rep[k]
    logprob = whole[1:2] - jnp.log(whole[0:1])
    chosen = lax.broadcasted_iota(jnp.int32, (samp, total_samp), 1) == (
        lax.broadcasted_iota(jnp.int32, (samp, total_samp), 0) + r * samp
    )
    own_rows = jnp.sum(jnp.where(chosen, logprob, 0.0), 1, keepdims=True)
    out[0:1] = as_row(own_rows, samp)
    for copy in sent:
        copy.wait_send()


def one_kernel(
    queries,
    new_keys,
    new_values,
    stored_keys,
    stored_values,
    lengths,
    out_proj,
    residual,
    norm_gain,
    embedding,
    targets,
    old_sums,
    rewards,
    group_ids,
):
    tps, reps = lax.axis_size("tp"), lax.axis_size("rep")
    samp, heads_kv, span, depth = stored_keys.shape
    heads = queries.shape[1] // depth
    total_samp = samp * reps
    cols = out_proj.shape[1]
    padded = (cols + 3 + 127) // 128 * 128
    share = total_samp // tps
    zs = reps // 2
    sends = (
        (zs - 1) + zs + (reps - 1) + (tps - 1) + (zs - 1) + zs * (tps - 1) + zs * tps
        + (tps - 1) + (reps - 1)
    )
    vmem = pl.BlockSpec(memory_space=pltpu.VMEM)
    hbm = pl.BlockSpec(memory_space=pltpu.HBM)
    dma = pltpu.SemaphoreType.DMA
    lanes_gain = norm_gain.reshape(-1, 128)
    sums = pl.pallas_call(
        functools.partial(step_kernel, tps, reps),
        out_shape=jax.ShapeDtypeStruct((2, samp), jnp.float32),
        in_specs=[hbm] * 13,
        out_specs=vmem,
        scratch_shapes=[
            pltpu.SMEM((samp,), jnp.int32),
            pltpu.VMEM(queries.shape, queries.dtype),
            pltpu.VMEM(new_keys.shape, new_keys.dtype),
            pltpu.VMEM(new_values.shape, new_values.dtype),
            pltpu.VMEM(residual.shape[::-1], residual.dtype),
            pltpu.VMEM(lanes_gain.shape, jnp.float32),
            pltpu.VMEM((1, total_samp), jnp.int32),
            pltpu.VMEM((1, samp), jnp.float32),
            pltpu.VMEM((1, samp), jnp.int32),
            pltpu.VMEM(stored_keys.shape, stored_keys.dtype),
            pltpu.VMEM(stored_values.shape, stored_values.dtype),
            pltpu.VMEM(out_proj.shape[::-1], out_proj.dtype),
            pltpu.VMEM((SLOTS, ROWS_PER_BLOCK, embedding.shape[1]), embedding.dtype),
            pltpu.VMEM((2, total_samp, ROWS_PER_BLOCK), jnp.float32),
            pltpu.VMEM((total_samp, 128), jnp.float32),
            pltpu.VMEM((total_samp, 128), jnp.float32),
            pltpu.VMEM((samp, heads, depth), jnp.float32),
            pltpu.VMEM((samp, heads, depth), jnp.float32),
            pltpu.VMEM((samp, heads, depth), jnp.float32),
            pltpu.VMEM((samp, heads, depth), jnp.float32),
            pltpu.VMEM((total_samp, heads * depth), jnp.bfloat16),
            pltpu.VMEM((tps, share, cols), jnp.bfloat16),
            pltpu.VMEM((tps, share, cols), jnp.bfloat16),
            pltpu.VMEM((tps, share, cols), jnp.float32),
            pltpu.VMEM((reps, total_samp, padded), jnp.bfloat16),
            pltpu.VMEM((total_samp, embedding.shape[1]), jnp.bfloat16),
            pltpu.VMEM((reps, 8, 128), jnp.float32),
            pltpu.VMEM((tps, 8, total_samp), jnp.float32),
            pltpu.VMEM((reps, 8, total_samp), jnp.float32),
            dma((12,)),
            dma((SLOTS,)),
            dma((sends,)),
            dma((reps,)),
            dma((tps,)),
            dma((tps * reps,)),
            dma((reps,)),
            dma((tps,)),
            dma((reps,)),
        ],
        compiler_params=pltpu.CompilerParams(
            collective_id=0, has_side_effects=True, vmem_limit_bytes=VMEM_BYTES
        ),
        name="decode_step",
    )(
        lengths,
        queries,
        new_keys,
        new_values,
        residual.T,
        lanes_gain,
        targets.reshape(1, -1),
        rewards.reshape(1, -1),
        group_ids.reshape(1, -1),
        stored_keys,
        stored_values,
        out_proj.T,
        embedding,
    )
    return old_sums + sums[0], rewards - (sums[1] - rewards) / (GROUP - 1.0)


def fits_one_kernel(tps, reps, stored_keys, out_proj, residual, embedding):
    samp, heads_kv, span, depth = stored_keys.shape
    total_samp = samp * reps
    return (
        span == 128
        and depth == 128
        and samp % 16 == 0
        and samp <= 128
        and reps % 2 == 0
        and total_samp == 128
        and total_samp % (16 * tps) == 0
        and 2 * out_proj.shape[1] % 128 == 0
        and out_proj.shape[1] % 16 == 0
        and embedding.shape[0] >= SLOTS * ROWS_PER_BLOCK
        and embedding.shape[0] % 16 == 0
        and embedding.shape[0] // ROWS_PER_BLOCK % 2 == 1
        and embedding.shape[1] == reps * out_proj.shape[1]
    )


def per_device_best(*args):
    tps, reps = lax.axis_size("tp"), lax.axis_size("rep")
    if fits_one_kernel(tps, reps, args[3], args[6], args[7], args[9]):
        return one_kernel(*args)
    return per_device(*args)


def solution(mesh):
    in_specs = (
        P("rep", "tp"),
        P("rep", "tp"),
        P("rep", "tp"),
        P("rep", "tp", None, None),
        P("rep", "tp", None, None),
        P("rep"),
        P("tp", "rep"),
        P(None, "rep"),
        P(),
        P(("tp", "rep"), None),
        P(),
        P("rep"),
        P("rep"),
        P("rep"),
    )
    out_specs = (P("rep"), P("rep"))
    return jax.shard_map(
        per_device_best, mesh=mesh, in_specs=in_specs, out_specs=out_specs, check_vma=False
    )
```
